512 devices in a mesh: sub: 2 (over core), row: 16 (over y, z_lo), col: 16 (over z_hi, x).
Axes of the slice: x: 4, y: 8, z: 8 (z_hi: 4, z_lo: 2; z = z_hi * 2 + z_lo), core: 2. Of those that a mesh axis runs over, the one named last changes fastest.
Arguments:
- front_entries: bfloat16 [5, 2, 16, 128, 10, 16, 128], P(None, 'sub', 'row', None, None, 'col'), may hold values from -6 to 6
- block_pattern: int32 [5, 2, 16, 10, 16], P(None, 'sub', 'row', None, 'col'), may hold values 0 or 1
- child_update: bfloat16 [2, 6, 16, 128, 6, 16, 128], P('sub', None, 'row', None, None, 'col'), may hold values from -6 to 6
- child_map: int32 [2, 6, 16], replicated, may hold values from 0 to 9, as said below
- diag_inverse: bfloat16 [1024, 1024], P('col'), may hold values from -0.0390625 to 0.0390625
Outputs:
- trailing: bfloat16 [5, 2, 16, 128, 10, 16, 128], P(None, 'sub', 'row', None, None, 'col')
The draws below stay inside these ranges and needn't reach their ends.
Inputs may be any that keep to these rules, and one draw needn't show every extreme that they name: For each child s and each r, the 6 values child_map[s, :, r] are distinct; exactly 3 of them are even and 3 odd.
All inputs are finite; a program needn't handle non-finite values. No bound on the sum of `block_pattern` on one device may be relied on, other than what follows from the above.
Results may differ from the reference program's by a relative error of at most 0.0057.
Values may be sent and summed in bfloat16 or wider, within the bound.
A program may use at most 64 MiB of HBM per device.

```python
import jax
import jax.numpy as jnp
from jax import lax

BLK = 128
PANEL = 1024
RBK = 5
CBK = 6
GRID = 16


def pick_targets(key):
    key_even, key_odd, key_order = jax.random.split(key, 3)
    even_slots = jax.random.permutation(key_even, RBK)[:CBK // 2] * 2
    odd_slots = jax.random.permutation(key_odd, RBK)[:CBK // 2] * 2 + 1
    joined = jnp.concatenate([even_slots, odd_slots]).astype(jnp.int32)
    return jax.random.permutation(key_order, joined)


def draw_child_map(key, part):
    key_list = jax.random.split(jax.random.fold_in(key, 7), 2 * GRID)
    slot_table = jax.vmap(pick_targets)(key_list)
    return slot_table.reshape(2, GRID, CBK).transpose(0, 2, 1).astype(jnp.int32)


def set_ends(values, rng, low, largest):
    index_at = [jax.random.randint(jax.random.fold_in(rng, axis), (), 0, length) for axis, length in enumerate(values.shape)]
    longest = values.shape.index(max(values.shape))
    beside = index_at[:longest] + [(index_at[longest] + 1) % values.shape[longest]] + index_at[longest + 1:]
    return values.at[tuple(index_at)].set(low).at[tuple(beside)].set(largest)


def block_scale(rng, shape, cuts, least, high):
    gain = 1.0
    for dim, parts in cuts:
        draws = jax.random.uniform(jax.random.fold_in(jax.random.fold_in(rng, 6), dim), (parts,), jnp.float32, least / len(cuts), high / len(cuts))
        gain = gain * jnp.repeat(jnp.exp(draws), shape[dim] // parts).reshape((-1,) + (1,) * (len(shape) - 1 - dim))
    return gain


def bell_draw(own_key, shape, width, reach, cuts=(), kind=jnp.bfloat16):
    drawn = jax.random.normal(own_key, shape, jnp.float32) * width
    if len(cuts) > 0:
        drawn = block_scale(own_key, shape, cuts, -0.22, 0.18) * drawn
    return jnp.clip(drawn, min=-reach, max=reach).astype(kind)


def setup_inputs(seed: int = 0) -> dict:
    arg_keys = jax.random.split(jax.random.key(seed), 6)
    return {
        "front_entries": bell_draw(arg_keys[0], (RBK, 2, GRID, BLK, 2 * RBK, GRID, BLK), 1.0, 6.0, ((1, 2), (2, 16), (5, 16))),
        "block_pattern": set_ends((jax.random.randint(arg_keys[1], (RBK, 2, GRID, 2 * RBK, GRID), 0, 2) < 1).astype(jnp.int32), jax.random.fold_in(arg_keys[1], 1), 0, 1),
        "child_update": bell_draw(arg_keys[2], (2, CBK, GRID, BLK, CBK, GRID, BLK), 1.0, 6.0, ((0, 2), (2, 16), (5, 16))),
        "child_map": draw_child_map(jax.random.fold_in(arg_keys[5], 71), 0),
        "diag_inverse": bell_draw(arg_keys[4], (PANEL, PANEL), (PANEL * PANEL // 45) ** -0.5, 0.0390625, ((0, 16),)),
    }


def reference(front_entries, block_pattern, child_update, child_map, diag_inverse):
    nblocks = 2 * RBK * GRID
    front_order = nblocks * BLK
    child_blocks = CBK * GRID
    blocks = front_entries.reshape(nblocks, BLK, nblocks, BLK).transpose(0, 2, 1, 3).astype(jnp.float32)
    blocks = blocks * block_pattern.reshape(nblocks, nblocks)[:, :, None, None].astype(jnp.float32)
    positions = jnp.arange(GRID, dtype=jnp.int32)
    for child_index in range(2):
        targets = (child_map[child_index] * GRID + positions[None, :]).reshape(child_blocks).astype(jnp.int32)
        update = child_update[child_index].reshape(child_blocks, BLK, child_blocks, BLK).transpose(0, 2, 1, 3).astype(jnp.float32)
        blocks = blocks.at[targets[:, None], targets[None, :]].add(update)
    front = blocks.transpose(0, 2, 1, 3).reshape(front_order, front_order).astype(jnp.bfloat16)
    lower_inverse = jnp.tril(diag_inverse)
    contract = (((1,), (1,)), ((), ()))
    factor = lax.dot_general(front[:, :PANEL], lower_inverse, contract, preferred_element_type=jnp.float32).astype(jnp.bfloat16)

    def one_block(block_index):
        row_block = lax.dynamic_slice_in_dim(front, block_index * BLK, BLK, 0)
        left_rows = lax.dynamic_slice_in_dim(factor, block_index * BLK, BLK, 0)
        product = lax.dot_general(left_rows, factor, contract, preferred_element_type=jnp.float32)
        return (row_block.astype(jnp.float32) - product).astype(jnp.bfloat16)

    trailing = lax.map(one_block, jnp.arange(nblocks, dtype=jnp.int32))
    return trailing.reshape(RBK, 2, GRID, BLK, 2 * RBK, GRID, BLK)
```

```python
import jax
import jax.numpy as jnp
from jax import lax
from jax.experimental import pallas as pl
from jax.experimental.pallas import tpu as pltpu
from jax.sharding import PartitionSpec as P

MESH = pl.DeviceIdType.MESH
F32 = jnp.float32
BF16 = jnp.bfloat16

BLK = 128
RBK = 5
MB = 10
CBK = 6
ROWS = RBK * BLK
PANEL = 1024
PIECES = 4
PR = ROWS // PIECES
NT = (((1,), (1,)), ((), ()))


def bitrev3(value):
    return (value % 2) * 4 + ((value // 2) % 2) * 2 + value // 4


def kernel(
    cmap, pattern, entries_hbm, child_hbm, inverse_hbm, out_hbm,
    child, entries, front, pack0, pack, got0, got, left, right, inv, diag, fleft, fright, outv,
    local_sem, pk_send, pk_recv, lz_send, lz_recv, lx_send, lx_recv, lp_sem,
    sc_send, sc_recv, pr_send, pr_recv, z_send, z_recv, x_send, x_recv,
    y_send, y_recv, h_send, h_recv, out_sem,
):
    s = lax.axis_index("sub")
    row = lax.axis_index("row")
    col = lax.axis_index("col")
    y, zl = row // 2, row % 2
    zh, x = col // 4, col % 4
    holder = zh < 2
    other = 1 - s

    def at_row(r):
        return {"row": r}

    def at_col(c):
        return {"col": c}

    mate = {"sub": other}
    z_up, z_down = at_col(((zh + 1) % 4) * 4 + x), at_col(((zh + 3) % 4) * 4 + x)
    z_swap = at_col((zh + 1 - 2 * (zh % 2)) * 4 + x)
    z_flip = at_col((3 - zh) * 4 + x)
    x_up, x_down = at_col(zh * 4 + (x + 1) % 4), at_col(zh * 4 + (x + 3) % 4)
    y_up, y_down = at_row(((y + 1) % 8) * 2 + zl), at_row(((y + 7) % 8) * 2 + zl)
    pair = at_row(y * 2 + 1 - zl)

    def slot_of(y_at, group):
        return bitrev3((y_at + 24 - 3 * (group // 2) - 6) % 8)

    send_y = (bitrev3(col % 8) + 3 * y + 6) % 8
    source = {"row": col, "col": slot_of(y, col)}

    def rdma(src, dst, send, recv, to):
        return pltpu.make_async_remote_copy(
            src_ref=src, dst_ref=dst, send_sem=send, recv_sem=recv, device_id=to, device_id_type=MESH
        )

    def landed(dst, send, recv):
        rdma(dst, dst, send, recv, mate).wait_recv()

    def each(n, fn):
        def step(i, carry):
            fn(i)
            return carry

        lax.fori_loop(0, n, step, 0)

    child_in = pltpu.make_async_copy(child_hbm, child, local_sem.at[0])
    entries_in = pltpu.make_async_copy(entries_hbm, entries, local_sem.at[1])
    inv_in = pltpu.make_async_copy(
        inverse_hbm.at[pl.ds(pl.multiple_of(s * 32, 32), 32)], inv.at[zh, x, s], local_sem.at[2]
    )
    child_in.start()
    inv_in.start()
    entries_in.start()

    barrier = pltpu.get_barrier_semaphore()
    for to in (mate, z_up, z_down, x_up, x_down, y_up, y_down, pair, source):
        pl.semaphore_signal(barrier, inc=1, device_id=to, device_id_type=MESH)

    own_row = [cmap[a, s, row] for a in range(CBK)]
    other_row = [cmap[a, other, row] for a in range(CBK)]

    def nth_rows(values, parity):
        found = [jnp.int32(0)] * 3
        count = jnp.int32(0)
        for a in range(CBK):
            hit = values[a] % 2 == parity
            for n in range(3):
                found[n] = jnp.where(hit & (count == n), jnp.int32(a), found[n])
            count = count + jnp.where(hit, jnp.int32(1), jnp.int32(0))
        return found

    def lookup(values, wanted):
        index, have = jnp.int32(0), jnp.float32(0)
        for n, value in enumerate(values):
            index = jnp.where(value == wanted, jnp.int32(n), index)
            have = jnp.where(value == wanted, jnp.float32(1), have)
        return index, have

    out_rows = nth_rows(own_row, other)
    own_cols = [cmap[b, s, col] for b in range(CBK)]
    first_col, _ = lookup(own_cols, jnp.int32(0))
    child_in.wait()
    for n in range(3):
        pack0[n] = child[out_rows[n], first_col]
        for b in range(CBK):
            pack[n, b] = child[out_rows[n], b]

    in_slots = [jnp.int32(-1)] * 3
    count = jnp.int32(0)
    for a in range(CBK):
        hit = other_row[a] % 2 == s
        for n in range(3):
            in_slots[n] = jnp.where(hit & (count == n), other_row[a], in_slots[n])
        count = count + jnp.where(hit, jnp.int32(1), jnp.int32(0))
    own_at = [lookup(own_row, 2 * k + s) for k in range(RBK)]
    other_at = [lookup(in_slots, 2 * k + s) for k in range(RBK)]

    inv_in.wait()
    pl.semaphore_wait(barrier, 8 + jnp.where(holder, 2, 0))

    pk0_copy = rdma(pack0, got0, pk_send.at[0], pk_recv.at[0], mate)
    pk_copy = rdma(pack, got, pk_send.at[1], pk_recv.at[1], mate)
    pk0_copy.start()
    pk_copy.start()

    mine = inv.at[zh, x, s]
    z_below, z_above, z_far = (zh + 3) % 4, (zh + 1) % 4, (zh + 2) % 4
    lz_up = rdma(mine, mine, lz_send.at[0], lz_recv.at[0], z_up)
    lz_down = rdma(mine, mine, lz_send.at[1], lz_recv.at[1], z_down)
    lz_up.start()
    lz_down.start()
    low_half = inv.at[z_below, x, s, pl.ds(0, 16)]
    high_half = inv.at[z_above, x, s, pl.ds(16, 16)]
    lz_up2 = rdma(low_half, low_half, lz_send.at[2], lz_recv.at[2], z_up)
    lz_down2 = rdma(high_half, high_half, lz_send.at[3], lz_recv.at[3], z_down)

    def block(k, m, own_b, own_f, theirs, theirs_f):
        a, have_a = own_at[k]
        n, have_n = other_at[k]
        scale = pattern[k, m].astype(F32)
        value = entries[k, m].astype(F32) * scale
        value = value + child[a, own_b].astype(F32) * (have_a * own_f)
        return (value + theirs(n).astype(F32) * (have_n * theirs_f)).astype(BF16)

    def columns(m):
        own_b, own_f = lookup([cmap[b, s, col] for b in range(CBK)], m)
        other_b, other_f = lookup([cmap[b, other, col] for b in range(CBK)], m)
        return own_b, own_f, other_b, other_f

    entries_in.wait()
    landed(got0, pk_send.at[0], pk_recv.at[0])

    first = jnp.where((zh == 1) | (zh == 2), 1, 0)
    slot_a = first * 4 + x
    slot_b = (1 - first) * 4 + x

    def piece(p):
        return pl.ds(pl.multiple_of(p * PR, 32), PR)

    def z_copy(which, p):
        ref = left.at[slot_a, piece(p)]
        if which == 0:
            return rdma(ref, ref, z_send.at[0, p], z_recv.at[0, p], z_swap)
        if which == 1:
            return rdma(ref, ref, z_send.at[1, p], z_recv.at[0, p], z_flip)
        return rdma(ref, ref, z_send.at[0, p], z_recv.at[1, p], z_swap)

    def x_copy(which, p):
        x_below, x_above = (x + 3) % 4, (x + 1) % 4
        slot, to = [
            (slot_a, x_up),
            (slot_a, x_down),
            (slot_b, x_up),
            (slot_b, x_down),
            (first * 4 + x_below, x_up),
            ((1 - first) * 4 + x_above, x_down),
        ][which]
        ref = left.at[slot, piece(p)]
        return rdma(ref, ref, x_send.at[which, p], x_recv.at[which, p], to)

    def x_landed(which, p):
        slot = [
            first * 4 + (x + 3) % 4,
            first * 4 + (x + 1) % 4,
            (1 - first) * 4 + (x + 3) % 4,
            (1 - first) * 4 + (x + 1) % 4,
            first * 4 + (x + 2) % 4,
            (1 - first) * 4 + (x + 2) % 4,
        ][which]
        landed(left.at[slot, piece(p)], x_send.at[which, p], x_recv.at[which, p])

    def scatter_copy(half, p):
        part = piece(2 * half + p)
        return rdma(
            left.at[slot_a, part], right.at[s, slot_a, part], sc_send.at[half, p], sc_recv.at[p],
            {"row": send_y * 2 + half, "col": row},
        )

    @pl.when(holder)
    def _():
        own_b, own_f, other_b, other_f = columns(jnp.int32(0))
        for k in range(RBK):
            left[slot_a, pl.ds(k * BLK, BLK)] = block(k, 0, own_b, own_f, lambda n: got0[n], other_f)

        def go(p):
            scatter_copy(0, p).start()
            scatter_copy(1, p).start()

        each(2, go)

        def go_left(p):
            z_copy(0, p).start()
            z_copy(1, p).start()
            x_copy(0, p).start()
            x_copy(1, p).start()

        each(PIECES, go_left)

    landed(inv.at[z_below, x, s], lz_send.at[0], lz_recv.at[0])
    lz_up2.start()
    landed(inv.at[z_above, x, s], lz_send.at[1], lz_recv.at[1])
    lz_down2.start()

    def a_here(p):
        landed(left.at[slot_a, piece(p)], z_send.at[0, p], z_recv.at[0, p])

    @pl.when(jnp.logical_not(holder))
    def _():
        def go(p):
            a_here(p)
            z_copy(2, p).start()
            x_copy(0, p).start()
            x_copy(1, p).start()

        each(PIECES, go)

    far = inv.at[z_far, x, s]
    landed(far.at[pl.ds(0, 16)], lz_send.at[2], lz_recv.at[2])
    landed(far.at[pl.ds(16, 16)], lz_send.at[3], lz_recv.at[3])

    def inv_group(group, x_at):
        if group == 0:
            return inv.at[pl.ds(0, 2), x_at, s, :, pl.ds(0, PANEL // 2)]
        return inv.at[pl.ds(2, 2), x_at, s]

    def lx_copy(which):
        group, x_at, to = [
            (0, x, x_up),
            (0, x, x_down),
            (1, x, x_up),
            (1, x, x_down),
            (0, (x + 3) % 4, x_up),
            (1, (x + 1) % 4, x_down),
        ][which]
        ref = inv_group(group, x_at)
        return rdma(ref, ref, lx_send.at[which], lx_recv.at[which], to)

    def lx_landed(which):
        group, x_at = [
            (0, (x + 3) % 4),
            (0, (x + 1) % 4),
            (1, (x + 3) % 4),
            (1, (x + 1) % 4),
            (0, (x + 2) % 4),
            (1, (x + 2) % 4),
        ][which]
        landed(inv_group(group, x_at), lx_send.at[which], lx_recv.at[which])

    for which in range(4):
        lx_copy(which).start()

    own_slot = slot_of(y, col)

    def turn(q):
        return (2 * zl + q) % 4

    def y_copy(up, d, q):
        slot = slot_of((y + 8 - (d - 1)) % 8 if up else (y + d - 1) % 8, col)
        ref = right.at[s, slot, piece(turn(q))]
        way = 0 if up else 1
        return rdma(
            ref, ref, y_send.at[way, d - 1, q], y_recv.at[way, d - 1, q], y_up if up else y_down
        )

    def y_landed(up, d, q):
        slot = slot_of((y + 8 - d) % 8 if up else (y + d) % 8, col)
        way = 0 if up else 1
        landed(
            right.at[s, slot, piece(turn(q))], y_send.at[way, d - 1, q], y_recv.at[way, d - 1, q]
        )

    def pair_copy(p):
        ref = right.at[s, own_slot, piece(2 * zl + p)]
        return rdma(ref, ref, pr_send.at[p], pr_recv.at[p], pair)

    def hand_copy(which):
        shift = [0, 7, 1, 6, 2, 5, 3][which]
        ref = right.at[s, slot_of((y + shift) % 8, col)]
        return rdma(ref, ref, h_send.at[which], h_recv.at[which], mate)

    def hand_half(which):
        half = (zl + which) % 2
        ref = right.at[s, slot_of((y + 4) % 8, col), pl.ds(pl.multiple_of(half * 2 * PR, 32), 2 * PR)]
        return rdma(ref, ref, h_send.at[7 + which], h_recv.at[7 + which], mate)

    def from_source(p):
        landed(right.at[s, own_slot, piece(2 * zl + p)], sc_send.at[0, p], sc_recv.at[p])
        pair_copy(p).start()
        y_copy(True, 1, p).start()
        y_copy(False, 1, p).start()

    each(2, from_source)

    def assemble(m):
        own_b, own_f, other_b, other_f = columns(m)
        for k in range(RBK):
            front[k, m] = block(k, m, own_b, own_f, lambda n: got[n, other_b], other_f)

    landed(got, pk_send.at[1], pk_recv.at[1])
    each(RBK, assemble)

    def b_ready(p):
        @pl.when(holder)
        def _():
            landed(left.at[slot_b, piece(p)], z_send.at[0, p], z_recv.at[0, p])

        @pl.when(jnp.logical_not(holder))
        def _():
            landed(left.at[slot_b, piece(p)], z_send.at[0, p], z_recv.at[1, p])

        x_copy(2, p).start()
        x_copy(3, p).start()

    each(PIECES, b_ready)

    def from_pair(p):
        landed(right.at[s, own_slot, piece(2 * (1 - zl) + p)], pr_send.at[p], pr_recv.at[p])
        y_copy(True, 1, p + 2).start()
        y_copy(False, 1, p + 2).start()

    each(2, from_pair)
    hand_copy(0).start()

    def x_pass(p):
        x_landed(0, p)
        x_copy(4, p).start()
        x_landed(3, p)
        x_copy(5, p).start()

    each(PIECES, x_pass)

    lx_landed(0)
    lx_copy(4).start()
    lx_landed(3)
    lx_copy(5).start()

    def y_pass(d):
        def go(q):
            y_landed(True, d, q)
            y_copy(True, d + 1, q).start()
            y_landed(False, d, q)
            y_copy(False, d + 1, q).start()

        return go

    each(PIECES, y_pass(1))
    hand_copy(1).start()
    hand_copy(2).start()

    each(RBK, lambda m: assemble(m + RBK))

    def x_rest(p):
        for which in (2, 1, 4, 5):
            x_landed(which, p)

    each(PIECES, x_rest)
    for which in (2, 1, 4, 5):
        lx_landed(which)
    inv_hand = rdma(inv.at[:, :, s], inv.at[:, :, s], lp_sem.at[0], lp_sem.at[1], mate)
    inv_hand.start()

    each(PIECES, y_pass(2))
    hand_copy(3).start()
    hand_copy(4).start()

    landed(inv.at[:, :, other], lp_sem.at[0], lp_sem.at[1])
    keep = lax.broadcasted_iota(jnp.int32, (256, 256), 0) >= lax.broadcasted_iota(jnp.int32, (256, 256), 1)
    for nb in range(4):
        tile = inv[nb, :, :, :, pl.ds(nb * 256, 256)].reshape(256, 256).astype(F32)
        diag[nb] = jnp.where(keep, tile, 0.0).astype(BF16)

    def weights(nb):
        if nb == 0:
            return diag[0]
        return jnp.concatenate(
            [inv[nb, :, :, :, pl.ds(0, nb * 256)].reshape(256, nb * 256), diag[nb]], axis=1
        )

    def y_last(q):
        y_landed(True, 3, q)
        y_copy(True, 4, q).start()
        y_landed(False, 3, q)

    def y_last2(q):
        y_landed(True, 3, q + 2)
        y_landed(False, 3, q + 2)
        y_copy(False, 4, q + 2).start()

    each(2, y_last)
    each(2, y_last2)
    hand_copy(5).start()
    hand_copy(6).start()

    def left_factor(t):
        part = pl.ds(pl.multiple_of(t * 320, 64), 320)
        for nb in range(4):
            lhs = jnp.concatenate([left[c, part] for c in range(2 * nb + 2)], axis=1)
            fleft[part, pl.ds(nb * 256, 256)] = lax.dot_general(
                lhs, weights(nb), NT, preferred_element_type=F32
            ).astype(BF16)

    each(2, left_factor)

    each(2, lambda q: y_landed(True, 4, q))
    hand_half(0).start()
    each(2, lambda q: y_landed(False, 4, q + 2))
    hand_half(1).start()

    for which, shift in enumerate([0, 7, 1, 6, 2, 5, 3]):
        landed(right.at[other, slot_of((y + shift) % 8, col)], h_send.at[which], h_recv.at[which])
    for which in range(2):
        half = (zl + which) % 2
        landed(
            right.at[other, slot_of((y + 4) % 8, col), pl.ds(pl.multiple_of(half * 2 * PR, 32), 2 * PR)],
            h_send.at[7 + which], h_recv.at[7 + which],
        )

    def out_copy(kk):
        cols = pl.ds(2 * kk, 2)
        return pltpu.make_async_copy(outv.at[:, cols], out_hbm.at[:, cols], out_sem.at[kk])

    def finish(kk):
        part = pl.ds(pl.multiple_of(kk * BLK, BLK), BLK)
        for nb in range(4):
            lhs = jnp.concatenate(
                [
                    jnp.concatenate([right[h, c, part] for c in range(2 * nb + 2)], axis=1)
                    for h in range(2)
                ],
                axis=0,
            )
            fright[:, pl.ds(nb * 256, 256)] = lax.dot_general(
                lhs, weights(nb), NT, preferred_element_type=F32
            ).astype(BF16)
        product = lax.dot_general(fleft[...], fright[...], NT, preferred_element_type=F32)
        for k in range(RBK):
            for h in range(2):
                tile = product[k * BLK:(k + 1) * BLK, h * BLK:(h + 1) * BLK]
                outv[k, 2 * kk + h] = (front[k, 2 * kk + h].astype(F32) - tile).astype(BF16)
        out_copy(kk).start()

    each(RBK, finish)
    each(RBK, lambda kk: out_copy(kk).wait())

    pk0_copy.wait_send()
    pk_copy.wait_send()
    for copy in (lz_up, lz_down, lz_up2, lz_down2, inv_hand):
        copy.wait_send()
    for which in range(6):
        lx_copy(which).wait_send()

    @pl.when(holder)
    def _():
        def done(p):
            scatter_copy(0, p).wait_send()
            scatter_copy(1, p).wait_send()

        each(2, done)

    def left_done(p):
        z_copy(0, p).wait_send()

        @pl.when(holder)
        def _():
            z_copy(1, p).wait_send()

        for which in range(6):
            x_copy(which, p).wait_send()
        for d in range(1, 4):
            y_copy(True, d, p).wait_send()
            y_copy(False, d, p).wait_send()

    each(PIECES, left_done)

    def last_done(p):
        pair_copy(p).wait_send()
        y_copy(True, 4, p).wait_send()
        y_copy(False, 4, p + 2).wait_send()

    each(2, last_done)
    for which in range(7):
        hand_copy(which).wait_send()
    for which in range(2):
        hand_half(which).wait_send()


def body(front_entries, block_pattern, child_update, child_map, diag_inverse):
    entries = front_entries.transpose(0, 4, 1, 2, 5, 3, 6).reshape(RBK, MB, BLK, BLK)
    child = child_update.transpose(0, 1, 4, 2, 5, 3, 6).reshape(CBK, CBK, BLK, BLK)
    pattern = block_pattern.reshape(RBK, MB)
    cmap = child_map.transpose(1, 0, 2)
    smem = pl.BlockSpec(memory_space=pltpu.SMEM)
    anyspace = pl.BlockSpec(memory_space=pl.ANY)
    dma = pltpu.SemaphoreType.DMA
    out = pl.pallas_call(
        kernel,
        out_shape=jax.ShapeDtypeStruct((RBK, MB, BLK, BLK), BF16),
        in_specs=[smem, smem, anyspace, anyspace, anyspace],
        out_specs=anyspace,
        scratch_shapes=[
            pltpu.VMEM((CBK, CBK, BLK, BLK), BF16),
            pltpu.VMEM((RBK, MB, BLK, BLK), BF16),
            pltpu.VMEM((RBK, MB, BLK, BLK), BF16),
            pltpu.VMEM((3, BLK, BLK), BF16),
            pltpu.VMEM((3, CBK, BLK, BLK), BF16),
            pltpu.VMEM((3, BLK, BLK), BF16),
            pltpu.VMEM((3, CBK, BLK, BLK), BF16),
            pltpu.VMEM((8, ROWS, BLK), BF16),
            pltpu.VMEM((2, 8, ROWS, BLK), BF16),
            pltpu.VMEM((4, 4, 2, 32, PANEL), BF16),
            pltpu.VMEM((4, 256, 256), BF16),
            pltpu.VMEM((ROWS, PANEL), BF16),
            pltpu.VMEM((2 * BLK, PANEL), BF16),
            pltpu.VMEM((RBK, MB, BLK, BLK), BF16),
            dma((3,)),
            dma((2,)), dma((2,)),
            dma((4,)), dma((4,)),
            dma((6,)), dma((6,)),
            dma((2,)),
            dma((2, 2)), dma((2,)),
            dma((2,)), dma((2,)),
            dma((2, PIECES)), dma((2, PIECES)),
            dma((6, PIECES)), dma((6, PIECES)),
            dma((2, 4, PIECES)), dma((2, 4, PIECES)),
            dma((9,)), dma((9,)),
            dma((RBK,)),
        ],
        compiler_params=pltpu.CompilerParams(
            collective_id=0, has_side_effects=True, vmem_limit_bytes=48 * 1024 * 1024
        ),
    )(cmap, pattern, entries, child, diag_inverse)
    out = out.reshape(RBK, MB, 1, 1, 1, BLK, BLK)
    return out.transpose(0, 2, 3, 5, 1, 4, 6)


def solution(mesh):
    return jax.shard_map(
        body,
        mesh=mesh,
        in_specs=(
            P(None, "sub", "row", None, None, "col", None),
            P(None, "sub", "row", None, "col"),
            P("sub", None, "row", None, None, "col", None),
            P(),
            P("col", None),
        ),
        out_specs=P(None, "sub", "row", None, None, "col", None),
        check_vma=False,
    )
```

```python
import jax
import jax.numpy as jnp
from jax import lax
from jax.experimental import pallas as pl
from jax.experimental.pallas import tpu as pltpu
from jax.sharding import PartitionSpec as P

MESH = pl.DeviceIdType.MESH
F32 = jnp.float32
BF16 = jnp.bfloat16

BLK = 128
RBK = 5
MB = 10
CBK = 6
ROWS = RBK * BLK
PANEL = 1024
PIECES = 4
PR = ROWS // PIECES
NT = (((1,), (1,)), ((), ()))


def bitrev3(value):
    return (value % 2) * 4 + ((value // 2) % 2) * 2 + value // 4


def kernel(
    cmap_hbm, pattern_hbm, entries_hbm, child_hbm, inverse_hbm, out_hbm,
    cmap, pattern,
    child, entries, front, pack0, pack, got0, got, left, right, inv, diag, fleft, fright, outv,
    local_sem, pk_send, pk_recv, lz_send, lz_recv, lx_send, lx_recv, lp_send, lp_recv,
    sc_send, sc_recv, pr_send, pr_recv, z_send, z_recv, x_send, x_recv,
    y_send, y_recv, h_send, h_recv, out_sem,
):
    s = lax.axis_index("sub")
    row = lax.axis_index("row")
    col = lax.axis_index("col")
    y, zl = row // 2, row % 2
    zh, x = col // 4, col % 4
    holder = zh < 2
    other = 1 - s

    def at_row(r):
        return {"row": r}

    def at_col(c):
        return {"col": c}

    mate = {"sub": other}
    z_up, z_down = at_col(((zh + 1) % 4) * 4 + x), at_col(((zh + 3) % 4) * 4 + x)
    z_swap = at_col((zh + 1 - 2 * (zh % 2)) * 4 + x)
    z_flip = at_col((3 - zh) * 4 + x)
    x_up, x_down = at_col(zh * 4 + (x + 1) % 4), at_col(zh * 4 + (x + 3) % 4)
    y_up, y_down = at_row(((y + 1) % 8) * 2 + zl), at_row(((y + 7) % 8) * 2 + zl)
    pair = at_row(y * 2 + 1 - zl)

    def slot_of(y_at, group):
        return bitrev3((y_at + 24 - 3 * (group // 2) - 6) % 8)

    send_y = (bitrev3(col % 8) + 3 * y + 6) % 8
    source = {"row": col, "col": slot_of(y, col)}

    def rdma(src, dst, send, recv, to):
        return pltpu.make_async_remote_copy(
            src_ref=src, dst_ref=dst, send_sem=send, recv_sem=recv, device_id=to, device_id_type=MESH
        )

    def landed(dst, send, recv):
        rdma(dst, dst, send, recv, mate).wait_recv()

    def each(n, fn):
        def step(i, carry):
            fn(i)
            return carry

        lax.fori_loop(0, n, step, 0)

    child_in = pltpu.make_async_copy(child_hbm, child, local_sem.at[0])
    entries_in = pltpu.make_async_copy(entries_hbm, entries, local_sem.at[1])
    inv_in = pltpu.make_async_copy(
        inverse_hbm.at[pl.ds(pl.multiple_of(s * 32, 32), 32)], inv.at[zh, x, s], local_sem.at[2]
    )
    cmap_in = pltpu.make_async_copy(cmap_hbm, cmap, local_sem.at[3])
    pattern_in = pltpu.make_async_copy(pattern_hbm, pattern, local_sem.at[4])
    cmap_in.start()
    child_in.start()
    inv_in.start()
    pattern_in.start()
    entries_in.start()

    barrier = pltpu.get_barrier_semaphore()
    for to in (mate, z_up, z_down, x_up, x_down, y_up, y_down, pair, source):
        pl.semaphore_signal(barrier, inc=1, device_id=to, device_id_type=MESH)

    cmap_in.wait()
    own_row = [cmap[a, s, row] for a in range(CBK)]
    other_row = [cmap[a, other, row] for a in range(CBK)]

    def nth_rows(values, parity):
        found = [jnp.int32(0)] * 3
        count = jnp.int32(0)
        for a in range(CBK):
            hit = values[a] % 2 == parity
            for n in range(3):
                found[n] = jnp.where(hit & (count == n), jnp.int32(a), found[n])
            count = count + jnp.where(hit, jnp.int32(1), jnp.int32(0))
        return found

    def lookup(values, wanted):
        index, have = jnp.int32(0), jnp.float32(0)
        for n, value in enumerate(values):
            index = jnp.where(value == wanted, jnp.int32(n), index)
            have = jnp.where(value == wanted, jnp.float32(1), have)
        return index, have

    out_rows = nth_rows(own_row, other)
    own_cols = [cmap[b, s, col] for b in range(CBK)]
    first_col, _ = lookup(own_cols, jnp.int32(0))
    child_in.wait()
    for n in range(3):
        pack0[n] = child[out_rows[n], first_col]
        for b in range(CBK):
            pack[n, b] = child[out_rows[n], b]

    in_slots = [jnp.int32(-1)] * 3
    count = jnp.int32(0)
    for a in range(CBK):
        hit = other_row[a] % 2 == s
        for n in range(3):
            in_slots[n] = jnp.where(hit & (count == n), other_row[a], in_slots[n])
        count = count + jnp.where(hit, jnp.int32(1), jnp.int32(0))
    own_at = [lookup(own_row, 2 * k + s) for k in range(RBK)]
    other_at = [lookup(in_slots, 2 * k + s) for k in range(RBK)]

    inv_in.wait()
    pl.semaphore_wait(barrier, 8 + jnp.where(holder, 2, 0))

    pk0_copy = rdma(pack0, got0, pk_send.at[0], pk_recv.at[0], mate)
    pk_copy = rdma(pack, got, pk_send.at[1], pk_recv.at[1], mate)

    mine = inv.at[zh, x, s]
    z_below, z_above, z_far = (zh + 3) % 4, (zh + 1) % 4, (zh + 2) % 4
    lz_up = rdma(mine, mine, lz_send.at[0], lz_recv.at[0], z_up)
    lz_down = rdma(mine, mine, lz_send.at[1], lz_recv.at[1], z_down)
    lz_up.start()
    lz_down.start()
    low_half = inv.at[z_below, x, s, pl.ds(0, 16)]
    high_half = inv.at[z_above, x, s, pl.ds(16, 16)]
    lz_up2 = rdma(low_half, low_half, lz_send.at[2], lz_recv.at[2], z_up)
    lz_down2 = rdma(high_half, high_half, lz_send.at[3], lz_recv.at[3], z_down)

    pk0_copy.start()
    pk_copy.start()

    def block(k, m, own_b, own_f, theirs, theirs_f):
        a, have_a = own_at[k]
        n, have_n = other_at[k]
        scale = pattern[k, 0, m].astype(F32)
        value = entries[k, m].astype(F32) * scale
        value = value + child[a, own_b].astype(F32) * (have_a * own_f)
        return (value + theirs(n).astype(F32) * (have_n * theirs_f)).astype(BF16)

    def columns(m):
        own_b, own_f = lookup([cmap[b, s, col] for b in range(CBK)], m)
        other_b, other_f = lookup([cmap[b, other, col] for b in range(CBK)], m)
        return own_b, own_f, other_b, other_f

    pattern_in.wait()
    entries_in.wait()
    landed(got0, pk_send.at[0], pk_recv.at[0])

    first = jnp.where((zh == 1) | (zh == 2), 1, 0)
    slot_a = first * 4 + x
    slot_b = (1 - first) * 4 + x

    def piece(p):
        return pl.ds(pl.multiple_of(p * PR, 32), PR)

    def z_copy(which, p):
        ref = left.at[slot_a, piece(p)]
        if which == 0:
            return rdma(ref, ref, z_send.at[0, p], z_recv.at[0, p], z_swap)
        if which == 1:
            return rdma(ref, ref, z_send.at[1, p], z_recv.at[0, p], z_flip)
        return rdma(ref, ref, z_send.at[0, p], z_recv.at[1, p], z_swap)

    def x_copy(which, p):
        x_below, x_above = (x + 3) % 4, (x + 1) % 4
        slot, to = [
            (slot_a, x_up),
            (slot_a, x_down),
            (slot_b, x_up),
            (slot_b, x_down),
            (first * 4 + x_below, x_up),
            ((1 - first) * 4 + x_above, x_down),
        ][which]
        ref = left.at[slot, piece(p)]
        return rdma(ref, ref, x_send.at[which, p], x_recv.at[which, p], to)

    def x_landed(which, p):
        slot = [
            first * 4 + (x + 3) % 4,
            first * 4 + (x + 1) % 4,
            (1 - first) * 4 + (x + 3) % 4,
            (1 - first) * 4 + (x + 1) % 4,
            first * 4 + (x + 2) % 4,
            (1 - first) * 4 + (x + 2) % 4,
        ][which]
        landed(left.at[slot, piece(p)], x_send.at[which, p], x_recv.at[which, p])

    def scatter_copy(half, p):
        part = piece(2 * half + p)
        return rdma(
            left.at[slot_a, part], right.at[s, slot_a, part], sc_send.at[half, p], sc_recv.at[p],
            {"row": send_y * 2 + half, "col": row},
        )

    def a_here(p):
        landed(left.at[slot_a, piece(p)], z_send.at[0, p], z_recv.at[0, p])

    far = inv.at[z_far, x, s]

    def inv_part(zq, x_at):
        return inv.at[zq, x_at, s, :, pl.ds(0, (zq + 1) * 256)]

    def lx_copy(kind, zq):
        if kind < 2:
            x_at, to = x, (x_up, x_down)[kind]
        elif zq in (0, 3):
            x_at, to = (x + 3) % 4, x_up
        else:
            x_at, to = (x + 1) % 4, x_down
        ref = inv_part(zq, x_at)
        return rdma(ref, ref, lx_send.at[kind, zq], lx_recv.at[kind, zq], to)

    def lx_landed(kind, zq):
        x_at = (x + (3, 1, 2)[kind]) % 4
        landed(inv_part(zq, x_at), lx_send.at[kind, zq], lx_recv.at[kind, zq])


    own_slot = slot_of(y, col)

    def turn(q):
        return (2 * zl + q) % 4

    def y_copy(up, d, q):
        slot = slot_of((y + 8 - (d - 1)) % 8 if up else (y + d - 1) % 8, col)
        ref = right.at[s, slot, piece(turn(q))]
        way = 0 if up else 1
        return rdma(
            ref, ref, y_send.at[way, d - 1, q], y_recv.at[way, d - 1, q], y_up if up else y_down
        )

    def y_landed(up, d, q):
        slot = slot_of((y + 8 - d) % 8 if up else (y + d) % 8, col)
        way = 0 if up else 1
        landed(
            right.at[s, slot, piece(turn(q))], y_send.at[way, d - 1, q], y_recv.at[way, d - 1, q]
        )

    def pair_copy(p):
        ref = right.at[s, own_slot, piece(2 * zl + p)]
        return rdma(ref, ref, pr_send.at[p], pr_recv.at[p], pair)

    def hand_copy(which):
        shift = [0, 7, 1, 6, 2, 5, 3][which]
        ref = right.at[s, slot_of((y + shift) % 8, col)]
        return rdma(ref, ref, h_send.at[which], h_recv.at[which], mate)

    def hand_half(which):
        half = (zl + which) % 2
        ref = right.at[s, slot_of((y + 4) % 8, col), pl.ds(pl.multiple_of(half * 2 * PR, 32), 2 * PR)]
        return rdma(ref, ref, h_send.at[7 + which], h_recv.at[7 + which], mate)

    def from_source(p):
        landed(right.at[s, own_slot, piece(2 * zl + p)], sc_send.at[0, p], sc_recv.at[p])
        pair_copy(p).start()
        y_copy(True, 1, p).start()
        y_copy(False, 1, p).start()

    def assemble(m):
        own_b, own_f, other_b, other_f = columns(m)
        for k in range(RBK):
            front[k, m] = block(k, m, own_b, own_f, lambda n: got[n, other_b], other_f)

    def b_ready(p):
        @pl.when(holder)
        def _():
            landed(left.at[slot_b, piece(p)], z_send.at[0, p], z_recv.at[0, p])

        @pl.when(jnp.logical_not(holder))
        def _():
            landed(left.at[slot_b, piece(p)], z_send.at[0, p], z_recv.at[1, p])

        x_copy(2, p).start()
        x_copy(3, p).start()

    def from_pair(p):
        landed(right.at[s, own_slot, piece(2 * (1 - zl) + p)], pr_send.at[p], pr_recv.at[p])
        y_copy(True, 1, p + 2).start()
        y_copy(False, 1, p + 2).start()

    def x_pass(p):
        x_landed(0, p)
        x_copy(4, p).start()
        x_landed(3, p)
        x_copy(5, p).start()

    def y_pass(d):
        def go(q):
            y_landed(True, d, q)
            y_copy(True, d + 1, q).start()
            y_landed(False, d, q)
            y_copy(False, d + 1, q).start()

        return go

    def x_rest(p):
        for which in (2, 1, 4, 5):
            x_landed(which, p)

    def weights(nb):
        if nb == 0:
            return diag[0]
        return jnp.concatenate(
            [inv[nb, :, :, :, pl.ds(0, nb * 256)].reshape(256, nb * 256), diag[nb]], axis=1
        )

    def y_last(q):
        y_landed(True, 3, q)
        y_copy(True, 4, q).start()
        y_landed(False, 3, q)

    def y_last2(q):
        y_landed(True, 3, q + 2)
        y_landed(False, 3, q + 2)
        y_copy(False, 4, q + 2).start()

    def left_factor(t):
        part = pl.ds(pl.multiple_of(t * 320, 64), 320)
        for nb in range(4):
            lhs = jnp.concatenate([left[c, part] for c in range(2 * nb + 2)], axis=1)
            fleft[part, pl.ds(nb * 256, 256)] = lax.dot_general(
                lhs, weights(nb), NT, preferred_element_type=F32
            ).astype(BF16)

    def inv_hand(zq, half):
        ref = inv.at[zq, :, half, :, pl.ds(0, (zq + 1) * 256)]
        return rdma(ref, ref, lp_send.at[zq], lp_recv.at[zq], mate)

    def go_scatter(p):
        scatter_copy(0, p).start()
        scatter_copy(1, p).start()

    def go_z(p):
        z_copy(0, p).start()
        z_copy(1, p).start()

    def go_xa(p):
        x_copy(0, p).start()
        x_copy(1, p).start()

    def relay_a(p):
        a_here(p)
        z_copy(2, p).start()
        x_copy(0, p).start()
        x_copy(1, p).start()

    def panel():
        own_b, own_f, other_b, other_f = columns(jnp.int32(0))
        for k in range(RBK):
            left[slot_a, pl.ds(k * BLK, BLK)] = block(k, 0, own_b, own_f, lambda n: got0[n], other_f)

    @pl.when(holder)
    def _():
        panel()
        each(2, go_scatter)
        each(PIECES, go_z)
        each(PIECES, go_xa)

    landed(inv.at[z_below, x, s], lz_send.at[0], lz_recv.at[0])
    lz_up2.start()
    landed(inv.at[z_above, x, s], lz_send.at[1], lz_recv.at[1])
    lz_down2.start()

    @pl.when(jnp.logical_not(holder))
    def _():
        each(PIECES, relay_a)

    each(2, from_source)

    each(PIECES, b_ready)

    each(2, from_pair)
    hand_copy(0).start()

    landed(far.at[pl.ds(0, 16)], lz_send.at[2], lz_recv.at[2])
    landed(far.at[pl.ds(16, 16)], lz_send.at[3], lz_recv.at[3])
    for zq in range(4):
        lx_copy(0, zq).start()
        lx_copy(1, zq).start()

    landed(got, pk_send.at[1], pk_recv.at[1])
    each(RBK, assemble)

    each(PIECES, x_pass)

    each(PIECES, y_pass(1))
    hand_copy(1).start()
    hand_copy(2).start()

    for zq in range(4):
        lx_landed(0 if zq in (0, 3) else 1, zq)
        lx_copy(2, zq).start()

    each(RBK, lambda m: assemble(m + RBK))

    each(PIECES, y_pass(2))
    hand_copy(3).start()
    hand_copy(4).start()

    each(PIECES, x_rest)

    for zq in range(4):
        lx_landed(1 if zq in (0, 3) else 0, zq)
        lx_landed(2, zq)
        inv_hand(zq, s).start()

    each(2, y_last)
    each(2, y_last2)
    hand_copy(5).start()
    hand_copy(6).start()

    for zq in range(4):
        landed(inv.at[zq, :, other, :, pl.ds(0, (zq + 1) * 256)], lp_send.at[zq], lp_recv.at[zq])
    keep = lax.broadcasted_iota(jnp.int32, (256, 256), 0) >= lax.broadcasted_iota(jnp.int32, (256, 256), 1)
    for nb in range(4):
        tile = inv[nb, :, :, :, pl.ds(nb * 256, 256)].reshape(256, 256).astype(F32)
        diag[nb] = jnp.where(keep, tile, 0.0).astype(BF16)


    each(2, left_factor)

    each(2, lambda q: y_landed(True, 4, q))
    hand_half(0).start()
    each(2, lambda q: y_landed(False, 4, q + 2))
    hand_half(1).start()

    for which, shift in enumerate([0, 7, 1, 6, 2, 5, 3]):
        landed(right.at[other, slot_of((y + shift) % 8, col)], h_send.at[which], h_recv.at[which])
    for which in range(2):
        half = (zl + which) % 2
        landed(
            right.at[other, slot_of((y + 4) % 8, col), pl.ds(pl.multiple_of(half * 2 * PR, 32), 2 * PR)],
            h_send.at[7 + which], h_recv.at[7 + which],
        )

    def out_copy(kk):
        cols = pl.ds(2 * kk, 2)
        return pltpu.make_async_copy(outv.at[:, cols], out_hbm.at[:, cols], out_sem.at[kk])

    def finish(kk):
        part = pl.ds(pl.multiple_of(kk * BLK, BLK), BLK)
        for nb in range(4):
            lhs = jnp.concatenate(
                [
                    jnp.concatenate([right[h, c, part] for c in range(2 * nb + 2)], axis=1)
                    for h in range(2)
                ],
                axis=0,
            )
            fright[:, pl.ds(nb * 256, 256)] = lax.dot_general(
                lhs, weights(nb), NT, preferred_element_type=F32
            ).astype(BF16)
        product = lax.dot_general(fleft[...], fright[...], NT, preferred_element_type=F32)
        for k in range(RBK):
            for h in range(2):
                tile = product[k * BLK:(k + 1) * BLK, h * BLK:(h + 1) * BLK]
                outv[k, 2 * kk + h] = (front[k, 2 * kk + h].astype(F32) - tile).astype(BF16)
        out_copy(kk).start()

    each(RBK, finish)
    each(RBK, lambda kk: out_copy(kk).wait())

    pk0_copy.wait_send()
    pk_copy.wait_send()
    for copy in (lz_up, lz_down, lz_up2, lz_down2):
        copy.wait_send()
    for zq in range(4):
        inv_hand(zq, s).wait_send()
    for kind in range(3):
        for zq in range(4):
            lx_copy(kind, zq).wait_send()

    @pl.when(holder)
    def _():
        def done(p):
            scatter_copy(0, p).wait_send()
            scatter_copy(1, p).wait_send()

        each(2, done)

    def left_done(p):
        z_copy(0, p).wait_send()

        @pl.when(holder)
        def _():
            z_copy(1, p).wait_send()

        for which in range(6):
            x_copy(which, p).wait_send()
        for d in range(1, 4):
            y_copy(True, d, p).wait_send()
            y_copy(False, d, p).wait_send()

    each(PIECES, left_done)

    def last_done(p):
        pair_copy(p).wait_send()
        y_copy(True, 4, p).wait_send()
        y_copy(False, 4, p + 2).wait_send()

    each(2, last_done)
    for which in range(7):
        hand_copy(which).wait_send()
    for which in range(2):
        hand_half(which).wait_send()


def body(front_entries, block_pattern, child_update, child_map, diag_inverse):
    entries = front_entries.transpose(0, 4, 1, 2, 5, 3, 6).reshape(RBK, MB, BLK, BLK)
    child = child_update.transpose(0, 1, 4, 2, 5, 3, 6).reshape(CBK, CBK, BLK, BLK)
    pattern = block_pattern.reshape(RBK, 1, MB)
    cmap = child_map.transpose(1, 0, 2)
    anyspace = pl.BlockSpec(memory_space=pl.ANY)
    hbm = pl.BlockSpec(memory_space=pltpu.HBM)
    dma = pltpu.SemaphoreType.DMA
    out = pl.pallas_call(
        kernel,
        out_shape=jax.ShapeDtypeStruct((RBK, MB, BLK, BLK), BF16),
        in_specs=[hbm] * 5,
        out_specs=anyspace,
        scratch_shapes=[
            pltpu.SMEM((CBK, 2, 16), jnp.int32),
            pltpu.SMEM((RBK, 1, MB), jnp.int32),
            pltpu.VMEM((CBK, CBK, BLK, BLK), BF16),
            pltpu.VMEM((RBK, MB, BLK, BLK), BF16),
            pltpu.VMEM((RBK, MB, BLK, BLK), BF16),
            pltpu.VMEM((3, BLK, BLK), BF16),
            pltpu.VMEM((3, CBK, BLK, BLK), BF16),
            pltpu.VMEM((3, BLK, BLK), BF16),
            pltpu.VMEM((3, CBK, BLK, BLK), BF16),
            pltpu.VMEM((8, ROWS, BLK), BF16),
            pltpu.VMEM((2, 8, ROWS, BLK), BF16),
            pltpu.VMEM((4, 4, 2, 32, PANEL), BF16),
            pltpu.VMEM((4, 256, 256), BF16),
            pltpu.VMEM((ROWS, PANEL), BF16),
            pltpu.VMEM((2 * BLK, PANEL), BF16),
            pltpu.VMEM((RBK, MB, BLK, BLK), BF16),
            dma((5,)),
            dma((2,)), dma((2,)),
            dma((4,)), dma((4,)),
            dma((3, 4)), dma((3, 4)),
            dma((4,)), dma((4,)),
            dma((2, 2)), dma((2,)),
            dma((2,)), dma((2,)),
            dma((2, PIECES)), dma((2, PIECES)),
            dma((6, PIECES)), dma((6, PIECES)),
            dma((2, 4, PIECES)), dma((2, 4, PIECES)),
            dma((9,)), dma((9,)),
            dma((RBK,)),
        ],
        compiler_params=pltpu.CompilerParams(
            collective_id=0, has_side_effects=True, vmem_limit_bytes=67043328
        ),
    )(cmap, pattern, entries, child, diag_inverse)
    out = out.reshape(RBK, MB, 1, 1, 1, BLK, BLK)
    return out.transpose(0, 2, 3, 5, 1, 4, 6)


def solution(mesh):
    return jax.shard_map(
        body,
        mesh=mesh,
        in_specs=(
            P(None, "sub", "row", None, None, "col", None),
            P(None, "sub", "row", None, "col"),
            P("sub", None, "row", None, None, "col", None),
            P(),
            P("col", None),
        ),
        out_specs=P(None, "sub", "row", None, None, "col", None),
        check_vma=False,
    )
```

```python
import jax
import jax.numpy as jnp
from jax import lax
from jax.experimental import pallas as pl
from jax.experimental.pallas import tpu as pltpu
from jax.sharding import PartitionSpec as P

MESH = pl.DeviceIdType.MESH
F32 = jnp.float32
BF16 = jnp.bfloat16

BLK = 128
RBK = 5
MB = 10
CBK = 6
ROWS = RBK * BLK
PANEL = 1024
PIECES = 4
HALF = PIECES // 2
PR = ROWS // PIECES
NT = (((1,), (1,)), ((), ()))


def bitrev3(value):
    return (value % 2) * 4 + ((value // 2) % 2) * 2 + value // 4


def kernel(
    cmap_hbm, pattern_hbm, entries_hbm, child_hbm, inverse_hbm, outv,
    cmap, pattern,
    child, entries, front, pack0, pack, got0, got, left, right, inv, diag, fleft, fright,
    local_sem, pk_send, pk_recv, lz_send, lz_recv, lx_send, lx_recv, lp_send, lp_recv,
    sc_send, sc_recv, pr_send, pr_recv, z_send, z_recv, x_send, x_recv,
    y_send, y_recv, h_send, h_recv,
):
    s = lax.axis_index("sub")
    row = lax.axis_index("row")
    col = lax.axis_index("col")
    y, zl = row // 2, row % 2
    zh, x = col // 4, col % 4
    holder = zh < 2
    other = 1 - s

    def at_row(r):
        return {"row": r}

    def at_col(c):
        return {"col": c}

    mate = {"sub": other}
    z_up, z_down = at_col(((zh + 1) % 4) * 4 + x), at_col(((zh + 3) % 4) * 4 + x)
    z_swap = at_col((zh + 1 - 2 * (zh % 2)) * 4 + x)
    z_flip = at_col((3 - zh) * 4 + x)
    x_up, x_down = at_col(zh * 4 + (x + 1) % 4), at_col(zh * 4 + (x + 3) % 4)
    y_up, y_down = at_row(((y + 1) % 8) * 2 + zl), at_row(((y + 7) % 8) * 2 + zl)
    pair = at_row(y * 2 + 1 - zl)

    def slot_of(y_at, group):
        return bitrev3((y_at + 24 - 3 * (group // 2) - 6) % 8)

    send_y = (bitrev3(col % 8) + 3 * y + 6) % 8
    source = {"row": col, "col": slot_of(y, col)}

    def rdma(src, dst, send, recv, to):
        return pltpu.make_async_remote_copy(
            src_ref=src, dst_ref=dst, send_sem=send, recv_sem=recv, device_id=to, device_id_type=MESH
        )

    def landed(dst, send, recv):
        rdma(dst, dst, send, recv, mate).wait_recv()

    def each(n, fn):
        def step(i, carry):
            fn(i)
            return carry

        lax.fori_loop(0, n, step, 0)

    child_in = pltpu.make_async_copy(child_hbm, child, local_sem.at[0])
    entries_in = pltpu.make_async_copy(entries_hbm, entries, local_sem.at[1])
    inv_in = pltpu.make_async_copy(
        inverse_hbm.at[pl.ds(pl.multiple_of(s * 32, 32), 32)], inv.at[zh, x, s], local_sem.at[2]
    )
    cmap_in = pltpu.make_async_copy(cmap_hbm, cmap, local_sem.at[3])
    pattern_in = pltpu.make_async_copy(pattern_hbm, pattern, local_sem.at[4])
    cmap_in.start()
    child_in.start()
    inv_in.start()
    pattern_in.start()
    entries_in.start()

    barrier = pltpu.get_barrier_semaphore()
    for to in (mate, z_up, z_down, x_up, x_down, y_up, y_down, pair, source):
        pl.semaphore_signal(barrier, inc=1, device_id=to, device_id_type=MESH)

    cmap_in.wait()
    own_row = [cmap[a, s, row] for a in range(CBK)]
    other_row = [cmap[a, other, row] for a in range(CBK)]

    def nth_rows(values, parity):
        found = [jnp.int32(0)] * 3
        count = jnp.int32(0)
        for a in range(CBK):
            hit = values[a] % 2 == parity
            for n in range(3):
                found[n] = jnp.where(hit & (count == n), jnp.int32(a), found[n])
            count = count + jnp.where(hit, jnp.int32(1), jnp.int32(0))
        return found

    def lookup(values, wanted):
        index, have = jnp.int32(0), jnp.float32(0)
        for n, value in enumerate(values):
            index = jnp.where(value == wanted, jnp.int32(n), index)
            have = jnp.where(value == wanted, jnp.float32(1), have)
        return index, have

    out_rows = nth_rows(own_row, other)
    own_cols = [cmap[b, s, col] for b in range(CBK)]
    first_col, _ = lookup(own_cols, jnp.int32(0))
    child_in.wait()
    for n in range(3):
        pack0[n] = child[out_rows[n], first_col]
        for b in range(CBK):
            pack[n, b] = child[out_rows[n], b]

    in_slots = [jnp.int32(-1)] * 3
    count = jnp.int32(0)
    for a in range(CBK):
        hit = other_row[a] % 2 == s
        for n in range(3):
            in_slots[n] = jnp.where(hit & (count == n), other_row[a], in_slots[n])
        count = count + jnp.where(hit, jnp.int32(1), jnp.int32(0))
    own_at = [lookup(own_row, 2 * k + s) for k in range(RBK)]
    other_at = [lookup(in_slots, 2 * k + s) for k in range(RBK)]

    inv_in.wait()
    pl.semaphore_wait(barrier, 8 + jnp.where(holder, 2, 0))

    pk0_copy = rdma(pack0, got0, pk_send.at[0], pk_recv.at[0], mate)
    pk_copy = rdma(pack, got, pk_send.at[1], pk_recv.at[1], mate)

    mine = inv.at[zh, x, s]
    z_below, z_above, z_far = (zh + 3) % 4, (zh + 1) % 4, (zh + 2) % 4
    lz_up = rdma(mine, mine, lz_send.at[0], lz_recv.at[0], z_up)
    lz_down = rdma(mine, mine, lz_send.at[1], lz_recv.at[1], z_down)
    lz_up.start()
    lz_down.start()
    low_half = inv.at[z_below, x, s, pl.ds(0, 16)]
    high_half = inv.at[z_above, x, s, pl.ds(16, 16)]
    lz_up2 = rdma(low_half, low_half, lz_send.at[2], lz_recv.at[2], z_up)
    lz_down2 = rdma(high_half, high_half, lz_send.at[3], lz_recv.at[3], z_down)

    pk0_copy.start()

    def block(k, m, own_b, own_f, theirs, theirs_f):
        a, have_a = own_at[k]
        n, have_n = other_at[k]
        scale = pattern[k, 0, m].astype(F32)
        value = entries[k, m].astype(F32) * scale
        value = value + child[a, own_b].astype(F32) * (have_a * own_f)
        return (value + theirs(n).astype(F32) * (have_n * theirs_f)).astype(BF16)

    def columns(m):
        own_b, own_f = lookup([cmap[b, s, col] for b in range(CBK)], m)
        other_b, other_f = lookup([cmap[b, other, col] for b in range(CBK)], m)
        return own_b, own_f, other_b, other_f

    pattern_in.wait()
    entries_in.wait()
    landed(got0, pk_send.at[0], pk_recv.at[0])
    pk_copy.start()

    first = jnp.where((zh == 1) | (zh == 2), 1, 0)
    slot_a = first * 4 + x
    slot_b = (1 - first) * 4 + x

    def piece(p):
        return pl.ds(pl.multiple_of(p * PR, 16), PR)

    def z_copy(which, p):
        ref = left.at[slot_a, piece(p)]
        if which == 0:
            return rdma(ref, ref, z_send.at[0, p], z_recv.at[0, p], z_swap)
        if which == 1:
            return rdma(ref, ref, z_send.at[1, p], z_recv.at[0, p], z_flip)
        return rdma(ref, ref, z_send.at[0, p], z_recv.at[1, p], z_swap)

    def x_copy(which, p):
        x_below, x_above = (x + 3) % 4, (x + 1) % 4
        slot, to = [
            (slot_a, x_up),
            (slot_a, x_down),
            (slot_b, x_up),
            (slot_b, x_down),
            (first * 4 + x_below, x_up),
            ((1 - first) * 4 + x_above, x_down),
        ][which]
        ref = left.at[slot, piece(p)]
        return rdma(ref, ref, x_send.at[which, p], x_recv.at[which, p], to)

    def x_landed(which, p):
        slot = [
            first * 4 + (x + 3) % 4,
            first * 4 + (x + 1) % 4,
            (1 - first) * 4 + (x + 3) % 4,
            (1 - first) * 4 + (x + 1) % 4,
            first * 4 + (x + 2) % 4,
            (1 - first) * 4 + (x + 2) % 4,
        ][which]
        landed(left.at[slot, piece(p)], x_send.at[which, p], x_recv.at[which, p])

    def scatter_copy(half, p):
        part = piece(HALF * half + p)
        return rdma(
            left.at[slot_a, part], right.at[s, slot_a, part], sc_send.at[half, p], sc_recv.at[p],
            {"row": send_y * 2 + half, "col": row},
        )

    def a_here(p):
        landed(left.at[slot_a, piece(p)], z_send.at[0, p], z_recv.at[0, p])

    far = inv.at[z_far, x, s]

    def inv_part(zq, x_at):
        return inv.at[zq, x_at, s, :, pl.ds(0, (zq + 1) * 256)]

    def lx_copy(kind, zq):
        if kind < 2:
            x_at, to = x, (x_up, x_down)[kind]
        elif zq in (0, 3):
            x_at, to = (x + 3) % 4, x_up
        else:
            x_at, to = (x + 1) % 4, x_down
        ref = inv_part(zq, x_at)
        return rdma(ref, ref, lx_send.at[kind, zq], lx_recv.at[kind, zq], to)

    def lx_landed(kind, zq):
        x_at = (x + (3, 1, 2)[kind]) % 4
        landed(inv_part(zq, x_at), lx_send.at[kind, zq], lx_recv.at[kind, zq])


    own_slot = slot_of(y, col)

    def turn(q):
        return (HALF * zl + q) % PIECES

    def y_copy(up, d, q):
        slot = slot_of((y + 8 - (d - 1)) % 8 if up else (y + d - 1) % 8, col)
        ref = right.at[s, slot, piece(turn(q))]
        way = 0 if up else 1
        return rdma(
            ref, ref, y_send.at[way, d - 1, q], y_recv.at[way, d - 1, q], y_up if up else y_down
        )

    def y_landed(up, d, q):
        slot = slot_of((y + 8 - d) % 8 if up else (y + d) % 8, col)
        way = 0 if up else 1
        landed(
            right.at[s, slot, piece(turn(q))], y_send.at[way, d - 1, q], y_recv.at[way, d - 1, q]
        )

    def pair_copy(p):
        ref = right.at[s, own_slot, piece(HALF * zl + p)]
        return rdma(ref, ref, pr_send.at[p], pr_recv.at[p], pair)

    def hand_copy(which):
        shift = [0, 7, 1, 6, 2, 5, 3][which]
        ref = right.at[s, slot_of((y + shift) % 8, col)]
        return rdma(ref, ref, h_send.at[which], h_recv.at[which], mate)

    def hand_half(which):
        half = (zl + which) % 2
        ref = right.at[s, slot_of((y + 4) % 8, col), pl.ds(pl.multiple_of(half * HALF * PR, 16), HALF * PR)]
        return rdma(ref, ref, h_send.at[7 + which], h_recv.at[7 + which], mate)

    def from_source(p):
        landed(right.at[s, own_slot, piece(HALF * zl + p)], sc_send.at[0, p], sc_recv.at[p])
        pair_copy(p).start()
        y_copy(True, 1, p).start()
        y_copy(False, 1, p).start()

    def assemble(m):
        own_b, own_f, other_b, other_f = columns(m)
        for k in range(RBK):
            front[k, m] = block(k, m, own_b, own_f, lambda n: got[n, other_b], other_f)

    def b_ready(p):
        @pl.when(holder)
        def _():
            landed(left.at[slot_b, piece(p)], z_send.at[0, p], z_recv.at[0, p])

        @pl.when(jnp.logical_not(holder))
        def _():
            landed(left.at[slot_b, piece(p)], z_send.at[0, p], z_recv.at[1, p])

        x_copy(2, p).start()
        x_copy(3, p).start()

    def from_pair(p):
        landed(right.at[s, own_slot, piece(HALF * (1 - zl) + p)], pr_send.at[p], pr_recv.at[p])
        y_copy(True, 1, p + HALF).start()
        y_copy(False, 1, p + HALF).start()

    def x_pass(p):
        x_landed(0, p)
        x_copy(4, p).start()
        x_landed(3, p)
        x_copy(5, p).start()

    def y_pass(d):
        def go(q):
            y_landed(True, d, q)
            y_copy(True, d + 1, q).start()
            y_landed(False, d, q)
            y_copy(False, d + 1, q).start()

        return go

    def x_rest(p):
        for which in (2, 1, 4, 5):
            x_landed(which, p)

    def weights(nb):
        if nb == 0:
            return diag[0]
        return jnp.concatenate(
            [inv[nb, :, :, :, pl.ds(0, nb * 256)].reshape(256, nb * 256), diag[nb]], axis=1
        )

    def y_last(q):
        y_landed(True, 3, q)
        y_copy(True, 4, q).start()
        y_landed(False, 3, q)

    def y_last2(q):
        y_landed(True, 3, q + HALF)
        y_landed(False, 3, q + HALF)
        y_copy(False, 4, q + HALF).start()

    def left_factor(t):
        part = pl.ds(pl.multiple_of(t * 320, 64), 320)
        for nb in range(4):
            lhs = jnp.concatenate([left[c, part] for c in range(2 * nb + 2)], axis=1)
            fleft[part, pl.ds(nb * 256, 256)] = lax.dot_general(
                lhs, weights(nb), NT, preferred_element_type=F32
            ).astype(BF16)

    def inv_hand(zq, half):
        ref = inv.at[zq, :, half, :, pl.ds(0, (zq + 1) * 256)]
        return rdma(ref, ref, lp_send.at[zq], lp_recv.at[zq], mate)

    def go_scatter(p):
        scatter_copy(0, p).start()
        scatter_copy(1, p).start()

    def go_z(p):
        z_copy(0, p).start()
        z_copy(1, p).start()

    def go_xa(p):
        x_copy(0, p).start()
        x_copy(1, p).start()

    def relay_a(p):
        a_here(p)
        z_copy(2, p).start()
        x_copy(0, p).start()
        x_copy(1, p).start()

    def panel():
        own_b, own_f, other_b, other_f = columns(jnp.int32(0))
        for k in range(RBK):
            left[slot_a, pl.ds(k * BLK, BLK)] = block(k, 0, own_b, own_f, lambda n: got0[n], other_f)

    @pl.when(holder)
    def _():
        panel()
        each(HALF, go_scatter)
        each(PIECES, go_z)
        each(PIECES, go_xa)

    landed(inv.at[z_below, x, s], lz_send.at[0], lz_recv.at[0])
    lz_up2.start()
    landed(inv.at[z_above, x, s], lz_send.at[1], lz_recv.at[1])
    lz_down2.start()

    @pl.when(jnp.logical_not(holder))
    def _():
        each(PIECES, relay_a)

    each(HALF, from_source)

    each(PIECES, b_ready)

    each(HALF, from_pair)
    hand_copy(0).start()

    landed(far.at[pl.ds(0, 16)], lz_send.at[2], lz_recv.at[2])
    landed(far.at[pl.ds(16, 16)], lz_send.at[3], lz_recv.at[3])
    for zq in range(4):
        lx_copy(0, zq).start()
        lx_copy(1, zq).start()

    landed(got, pk_send.at[1], pk_recv.at[1])
    each(RBK, assemble)

    each(PIECES, x_pass)

    each(PIECES, y_pass(1))
    hand_copy(1).start()
    hand_copy(2).start()

    for zq in range(4):
        lx_landed(0 if zq in (0, 3) else 1, zq)
        lx_copy(2, zq).start()

    each(RBK, lambda m: assemble(m + RBK))

    each(PIECES, y_pass(2))
    hand_copy(3).start()
    hand_copy(4).start()

    each(PIECES, x_rest)

    for zq in range(4):
        lx_landed(1 if zq in (0, 3) else 0, zq)
        lx_landed(2, zq)
        inv_hand(zq, s).start()

    each(HALF, y_last)
    each(HALF, y_last2)
    hand_copy(5).start()
    hand_copy(6).start()

    for zq in range(4):
        landed(inv.at[zq, :, other, :, pl.ds(0, (zq + 1) * 256)], lp_send.at[zq], lp_recv.at[zq])
    keep = lax.broadcasted_iota(jnp.int32, (256, 256), 0) >= lax.broadcasted_iota(jnp.int32, (256, 256), 1)
    for nb in range(4):
        tile = inv[nb, :, :, :, pl.ds(nb * 256, 256)].reshape(256, 256).astype(F32)
        diag[nb] = jnp.where(keep, tile, 0.0).astype(BF16)


    each(2, left_factor)

    each(HALF, lambda q: y_landed(True, 4, q))
    hand_half(0).start()
    each(HALF, lambda q: y_landed(False, 4, q + HALF))
    hand_half(1).start()

    def right_factor(half):
        def go(t):
            part = pl.ds(pl.multiple_of(t * 320, 64), 320)
            for nb in range(4):
                lhs = jnp.concatenate([right[half, c, part] for c in range(2 * nb + 2)], axis=1)
                fright[half, part, pl.ds(nb * 256, 256)] = lax.dot_general(
                    lhs, weights(nb), NT, preferred_element_type=F32
                ).astype(BF16)

        return go

    each(2, right_factor(s))

    for which, shift in enumerate([0, 7, 1, 6, 2, 5, 3]):
        landed(right.at[other, slot_of((y + shift) % 8, col)], h_send.at[which], h_recv.at[which])
    for which in range(2):
        half = (zl + which) % 2
        landed(
            right.at[other, slot_of((y + 4) % 8, col), pl.ds(pl.multiple_of(half * HALF * PR, 16), HALF * PR)],
            h_send.at[7 + which], h_recv.at[7 + which],
        )

    each(2, right_factor(other))

    def finish(kk):
        part = pl.ds(pl.multiple_of(kk * BLK, BLK), BLK)
        both = jnp.concatenate([fright[0, part], fright[1, part]], axis=0)
        product = lax.dot_general(fleft[...], both, NT, preferred_element_type=F32)
        for k in range(RBK):
            for h in range(2):
                tile = product[k * BLK:(k + 1) * BLK, h * BLK:(h + 1) * BLK]
                outv[k, 2 * kk + h] = (front[k, 2 * kk + h].astype(F32) - tile).astype(BF16)

    each(RBK, finish)

    pk0_copy.wait_send()
    pk_copy.wait_send()
    for copy in (lz_up, lz_down, lz_up2, lz_down2):
        copy.wait_send()
    for zq in range(4):
        inv_hand(zq, s).wait_send()
    for kind in range(3):
        for zq in range(4):
            lx_copy(kind, zq).wait_send()

    @pl.when(holder)
    def _():
        def done(p):
            scatter_copy(0, p).wait_send()
            scatter_copy(1, p).wait_send()

        each(HALF, done)

    def left_done(p):
        z_copy(0, p).wait_send()

        @pl.when(holder)
        def _():
            z_copy(1, p).wait_send()

        for which in range(6):
            x_copy(which, p).wait_send()
        for d in range(1, 4):
            y_copy(True, d, p).wait_send()
            y_copy(False, d, p).wait_send()

    each(PIECES, left_done)

    def last_done(p):
        pair_copy(p).wait_send()
        y_copy(True, 4, p).wait_send()
        y_copy(False, 4, p + HALF).wait_send()

    each(HALF, last_done)
    for which in range(7):
        hand_copy(which).wait_send()
    for which in range(2):
        hand_half(which).wait_send()


def body(front_entries, block_pattern, child_update, child_map, diag_inverse):
    entries = front_entries.transpose(0, 4, 1, 2, 5, 3, 6).reshape(RBK, MB, BLK, BLK)
    child = child_update.transpose(0, 1, 4, 2, 5, 3, 6).reshape(CBK, CBK, BLK, BLK)
    pattern = block_pattern.reshape(RBK, 1, MB)
    cmap = child_map.transpose(1, 0, 2)
    hbm = pl.BlockSpec(memory_space=pltpu.HBM)
    dma = pltpu.SemaphoreType.DMA
    entries, child, pattern, cmap, diag_inverse = (
        pltpu.with_memory_space_constraint(v, pltpu.HBM) for v in (entries, child, pattern, cmap, diag_inverse)
    )
    out = pl.pallas_call(
        kernel,
        out_shape=jax.ShapeDtypeStruct((RBK, MB, BLK, BLK), BF16),
        in_specs=[hbm] * 5,
        out_specs=pl.BlockSpec(memory_space=pltpu.VMEM),
        scratch_shapes=[
            pltpu.SMEM((CBK, 2, 16), jnp.int32),
            pltpu.SMEM((RBK, 1, MB), jnp.int32),
            pltpu.VMEM((CBK, CBK, BLK, BLK), BF16),
            pltpu.VMEM((RBK, MB, BLK, BLK), BF16),
            pltpu.VMEM((RBK, MB, BLK, BLK), BF16),
            pltpu.VMEM((3, BLK, BLK), BF16),
            pltpu.VMEM((3, CBK, BLK, BLK), BF16),
            pltpu.VMEM((3, BLK, BLK), BF16),
            pltpu.VMEM((3, CBK, BLK, BLK), BF16),
            pltpu.VMEM((8, ROWS, BLK), BF16),
            pltpu.VMEM((2, 8, ROWS, BLK), BF16),
            pltpu.VMEM((4, 4, 2, 32, PANEL), BF16),
            pltpu.VMEM((4, 256, 256), BF16),
            pltpu.VMEM((ROWS, PANEL), BF16),
            pltpu.VMEM((2, ROWS, PANEL), BF16),
            dma((5,)),
            dma((2,)), dma((2,)),
            dma((4,)), dma((4,)),
            dma((3, 4)), dma((3, 4)),
            dma((4,)), dma((4,)),
            dma((2, HALF)), dma((HALF,)),
            dma((HALF,)), dma((HALF,)),
            dma((2, PIECES)), dma((2, PIECES)),
            dma((6, PIECES)), dma((6, PIECES)),
            dma((2, 4, PIECES)), dma((2, 4, PIECES)),
            dma((9,)), dma((9,)),
        ],
        compiler_params=pltpu.CompilerParams(
            collective_id=0, has_side_effects=True, vmem_limit_bytes=52000000
        ),
    )(cmap, pattern, entries, child, diag_inverse)
    out = out.reshape(RBK, MB, 1, 1, 1, BLK, BLK)
    return out.transpose(0, 2, 3, 5, 1, 4, 6)


def solution(mesh):
    return jax.shard_map(
        body,
        mesh=mesh,
        in_specs=(
            P(None, "sub", "row", None, None, "col", None),
            P(None, "sub", "row", None, "col"),
            P("sub", None, "row", None, None, "col", None),
            P(),
            P("col", None),
        ),
        out_specs=P(None, "sub", "row", None, None, "col", None),
        check_vma=False,
    )
```
